32 devices in a mesh: market: 2 (over y), job: 4 (over z), worker: 4 (over x, core).
Axes of the slice: x: 2, y: 2, z: 4, core: 2. Of those that a mesh axis runs over, the one named last changes fastest.
Arguments:
- worker_feat: bfloat16 [8192, 128], P(('market', 'worker', 'job')), parts along dimension 0, may hold values from -164 to 164
- job_feat: bfloat16 [8192, 128], P(('market', 'job', 'worker')), parts along dimension 0, may hold values from -164 to 164
- affinity: bfloat16 [128, 128], replicated, may hold values from -0.046875 to 0.046875
- worker_mass: float32 [8192], P(('market', 'worker')), parts along dimension 0, may hold values from 0.25 to 4
- job_mass: float32 [8192], P(('market', 'job')), parts along dimension 0, may hold values from 0.25 to 4
- v_start: float32 [8192], P(('market', 'job')), parts along dimension 0, may hold values from -6 to 6
- observed: float32 [256, 128], P('market'), parts along dimension 0, may hold values from -1.5 to 1.5
Outputs:
- gradient: float32 [256, 128], P('market'), parts along dimension 0
- worker_potential: float32 [8192], P(('market', 'worker')), parts along dimension 0
- job_potential: float32 [8192], P(('market', 'job')), parts along dimension 0
The draws below stay inside these ranges and needn't reach their ends.
There are 2 independent parts, one for each index of `market`. The reference program is written for one: setup_inputs(seed, part) draws one part's arguments, and reference() takes and returns one part's arrays. A program takes and returns all parts, laid end to end along the dimension named above; an argument that names none is the same for every part. Nothing has to cross between parts.
All inputs are finite; a program needn't handle non-finite values.
Results may differ from the reference program's by a relative error of at most 0.0003.
The reference program's roundings to bfloat16 on the way (of `projected` and `coupling`) count: a program that leaves them out, or rounds other values in their place, can miss the bound.
Values may be sent and summed in bfloat16 or wider, within the bound.
No kernel may reach another device: no remote copies, remote signals or barrier semaphores. Data moves between devices by JAX's collectives and lax.ppermute only.
A program may use at most 64 MiB of HBM per device.

```python
import math
import jax
import jax.numpy as jnp
from jax import lax

K = 128
SWEEPS = 3
NW = 4096
NJ = 4096


def draw_features(key, rows):
    key_body = jax.random.fold_in(key, 0)
    values = jnp.clip(jax.random.normal(key_body, (rows, K), jnp.float32), -5.0, 5.0)
    return values.astype(jnp.bfloat16)


def draw_worker_feat(key, part):
    return draw_features(jax.random.fold_in(key, 11), NW)


def draw_job_feat(key, part):
    return draw_features(jax.random.fold_in(key, 23), NJ)


def levels(rng, shape, cuts, low, high):
    loudness, own = 1.0, jax.random.fold_in(rng, 6)
    for position, parts in cuts:
        steps = jnp.exp(jax.random.uniform(jax.random.fold_in(own, position), (parts,), jnp.float32, low / len(cuts), high / len(cuts)))
        loudness = loudness * jnp.repeat(steps, shape[position] // parts).reshape([-1 if axis == position else 1 for axis in range(len(shape))])
    return loudness


def noise(rng, shape, scale, limit, cuts=(), held_as=jnp.bfloat16):
    gain = levels(rng, shape, cuts, -0.22, 0.18) if cuts else 1.0
    values = jax.random.normal(rng, shape, jnp.float32) * scale * gain
    return jnp.minimum(jnp.maximum(values, -limit), limit).astype(held_as)


def setup_inputs(seed: int = 0, part: int = 0) -> dict:
    arg_keys = jax.random.split(jax.random.key(seed), 8)
    own_keys = jax.random.split(jax.random.fold_in(arg_keys[7], part), 8)
    return {
        "worker_feat": draw_worker_feat(jax.random.fold_in(jax.random.fold_in(arg_keys[7], part), 71), part),
        "job_feat": draw_job_feat(jax.random.fold_in(jax.random.fold_in(arg_keys[7], part), 71), part),
        "affinity": noise(arg_keys[2], (K, K), (K * K) ** -0.5, 0.046875),
        "worker_mass": jnp.clip(jnp.exp(math.log(4.0) - 2.7725887 * jax.random.uniform(own_keys[3], (NW,), jnp.float32) ** levels(own_keys[3], (NW,), ((0, 4),), -0.2, 0.2)), 0.25, 4.0),
        "job_mass": jnp.clip(jnp.exp(math.log(4.0) - 2.7725887 * jax.random.uniform(own_keys[4], (NJ,), jnp.float32) ** levels(own_keys[4], (NJ,), ((0, 4),), -0.2, 0.2)), 0.25, 4.0),
        "v_start": noise(own_keys[5], (NJ,), 1.0, 6.0, ((0, 4),), jnp.float32),
        "observed": noise(own_keys[6], (K, K), 0.1, 1.5, (), jnp.float32),
    }


block_rows = 512


def lse_combine(former, latter):
    highest = jnp.maximum(former[0], latter[0])
    return highest, former[1] * jnp.exp(former[0] - highest) + latter[1] * jnp.exp(latter[0] - highest)


def reference(worker_feat, job_feat, affinity, worker_mass, job_mass, v_start, observed):
    block_size = math.gcd(NW, block_rows)
    block_count = NW // block_size
    projected = jnp.dot(worker_feat, affinity, preferred_element_type=jnp.float32).astype(jnp.bfloat16)
    proj_blocks = projected.reshape(block_count, block_size, K)
    feat_blocks = worker_feat.reshape(block_count, block_size, K)
    log_worker = jnp.log(worker_mass) - jnp.log(jnp.sum(worker_mass))
    log_job = jnp.log(job_mass) - jnp.log(jnp.sum(job_mass))

    def surplus(row_block):
        return lax.dot_general(row_block, job_feat, (((1,), (1,)), ((), ())), preferred_element_type=jnp.float32)

    pot_v = v_start
    pot_u = jnp.zeros((NW,), jnp.float32)
    for sweep_index in range(SWEEPS):
        def row_lse(row_block, current=pot_v):
            scores = surplus(row_block) + current[None, :]
            highest = jnp.max(scores, axis=1)
            return highest + jnp.log(jnp.sum(jnp.exp(scores - highest[:, None]), axis=1))

        pot_u = log_worker - lax.map(row_lse, proj_blocks).reshape(NW)
        u_blocks = pot_u.reshape(block_count, block_size)

        def col_step(running, pieces):
            scores = surplus(pieces[0]) + pieces[1][:, None]
            highest = jnp.max(scores, axis=0)
            totals = jnp.sum(jnp.exp(scores - highest[None, :]), axis=0)
            return lse_combine(running, (highest, totals)), None

        start_state = (jnp.full((NJ,), -jnp.inf, jnp.float32), jnp.zeros((NJ,), jnp.float32))
        (highest, totals), _ = lax.scan(col_step, start_state, (proj_blocks, u_blocks))
        pot_v = log_job - (highest + jnp.log(totals))

    u_blocks = pot_u.reshape(block_count, block_size)

    def moment_step(running, pieces):
        coupling = jnp.exp(surplus(pieces[0]) + pieces[2][:, None] + pot_v[None, :]).astype(jnp.bfloat16)
        weighted = jnp.dot(coupling, job_feat, preferred_element_type=jnp.float32)
        term = lax.dot_general(pieces[1].astype(jnp.float32), weighted, (((0,), (0,)), ((), ())), precision=lax.Precision.HIGHEST)
        return running + term, None

    moment, _ = lax.scan(moment_step, jnp.zeros((K, K), jnp.float32), (proj_blocks, feat_blocks, u_blocks))
    return moment - observed, pot_u, pot_v
```

```python
import jax
import jax.numpy as jnp
from jax import lax
from jax.sharding import PartitionSpec as P

SWEEPS = 3


def parts_of(value, axis, size):
    if size & (size - 1) or size > 8:
        gathered = lax.all_gather(value, axis)
        return [gathered[k] for k in range(size)]
    return [value] + [
        lax.ppermute(value, axis, [(i, i ^ step) for i in range(size)]) for step in range(1, size)
    ]


def combine(pieces):
    highest = pieces[0]
    for piece in pieces[1:]:
        highest = jnp.maximum(highest, piece)
    total = sum(jnp.exp(piece - highest) for piece in pieces)
    return highest + jnp.log(total)


def local_lse(scores, axis):
    highest = jnp.max(scores, axis=axis, keepdims=True)
    return jnp.squeeze(highest, axis) + jnp.log(jnp.sum(jnp.exp(scores - highest), axis=axis))


def make(jobs, workers):
    def gather_sum(value, axis, size):
        return sum(parts_of(value, axis, size))

    def on_device(worker_feat, job_feat, affinity, worker_mass, job_mass, v_start, observed):
        jobs_local = lax.all_gather(job_feat, "worker", axis=0, tiled=True)
        workers_local = lax.all_gather(worker_feat, "job", axis=0, tiled=True)
        projected = jnp.dot(workers_local, affinity, preferred_element_type=jnp.float32).astype(
            jnp.bfloat16
        )
        worker_sum = gather_sum(jnp.sum(worker_mass).reshape(1, 1), "worker", workers)
        job_sum = gather_sum(jnp.sum(job_mass).reshape(1, 1), "job", jobs)
        log_worker = jnp.log(worker_mass) - jnp.log(worker_sum[0])
        log_job = jnp.log(job_mass) - jnp.log(job_sum[0])

        tile = lax.dot_general(
            projected, jobs_local, (((1,), (1,)), ((), ())), preferred_element_type=jnp.float32
        )
        pot_v = v_start
        pot_u = log_worker
        for sweep_index in range(SWEEPS):
            rows = local_lse(tile + pot_v[None, :], 1)
            pot_u = log_worker - combine(parts_of(rows, "job", jobs))
            columns = local_lse(tile + pot_u[:, None], 0)
            pot_v = log_job - combine(parts_of(columns, "worker", workers))
        coupling = jnp.exp(tile + pot_u[:, None] + pot_v[None, :]).astype(jnp.bfloat16)
        weighted = jnp.dot(coupling, jobs_local, preferred_element_type=jnp.float32)
        local_moment = lax.dot_general(
            workers_local.astype(jnp.float32),
            weighted,
            (((0,), (0,)), ((), ())),
            precision=lax.Precision.HIGHEST,
        )
        moment = gather_sum(gather_sum(local_moment, "worker", workers), "job", jobs)
        return (moment - observed, pot_u, pot_v)

    return on_device


def solution(mesh):
    placed = (
        P(("market", "worker", "job"), None),
        P(("market", "job", "worker"), None),
        P(),
        P(("market", "worker")),
        P(("market", "job")),
        P(("market", "job")),
        P("market", None),
    )
    return jax.shard_map(
        make(mesh.shape["job"], mesh.shape["worker"]),
        mesh=mesh,
        in_specs=placed,
        out_specs=(P("market", None), P(("market", "worker")), P(("market", "job"))),
        check_vma=False,
    )
```

```python
import functools

import jax
import jax.numpy as jnp
from jax import lax
from jax.experimental import pallas as pl
from jax.experimental.pallas import tpu as pltpu
from jax.sharding import PartitionSpec as P

SWEEPS = 3
LANES = 128
TILE = 512
CHUNK = 1024
BY_ROW = (((1,), (1,)), ((), ()))
BY_COLUMN = (((0,), (0,)), ((), ()))
F32 = jnp.float32
BF16 = jnp.bfloat16


def swap(value, axis, size, mask):
    return lax.ppermute(value, axis, [(i, i ^ mask) for i in range(size)])


def widen(value, width):
    return jnp.tile(value, (1, width // LANES))


def merged(pieces):
    highest = functools.reduce(jnp.maximum, pieces)
    return highest + jnp.log(sum(jnp.exp(piece - highest) for piece in pieces))


def new_v(col, pieces):
    cols = col.shape[1]
    both = merged(pieces)
    log_total = both[:, cols : cols + 1]
    return col + log_total - both[:, :cols], log_total


def scores_of(proj_ref, jobs_ref, at):
    return lax.dot_general(
        proj_ref[...], jobs_ref[pl.ds(at, TILE), :], BY_ROW, preferred_element_type=F32
    )


def sweep_rows_and_columns(proj_ref, jobs_ref, v_ref, shift_ref, mass_ref, out_ref, fresh_ref, scratch):
    e_ref, sum_ref, gain_ref = scratch
    rows, cols = proj_ref.shape[0], jobs_ref.shape[0]

    def fast(k, carry):
        at = pl.multiple_of(k * TILE, TILE)
        z = scores_of(proj_ref, jobs_ref, at) + v_ref[:, pl.ds(at, TILE)]
        if shift_ref is not None:
            z = z + widen(shift_ref[...], TILE)
        e = jnp.exp(z)
        e_ref[:, pl.ds(at, TILE)] = e
        part = e[:, :LANES]
        for j in range(1, TILE // LANES):
            part = part + e[:, j * LANES : (j + 1) * LANES]
        sum_ref[...] = sum_ref[...] + part
        return carry

    sum_ref[...] = jnp.zeros_like(sum_ref)
    lax.fori_loop(0, cols // TILE, fast, 0, unroll=True)
    total = jnp.sum(sum_ref[...], axis=1, keepdims=True)
    gain_ref[...] = mass_ref[...] / total
    fresh = jnp.log(gain_ref[...])
    fresh_ref[...] = fresh if shift_ref is None else shift_ref[...] + fresh
    least = jnp.full((1, CHUNK), jnp.inf, F32)
    for k in range(cols // CHUNK):
        span = slice(k * CHUNK, (k + 1) * CHUNK)
        acc = jnp.zeros((8, CHUNK), F32)
        for i in range(rows // 8):
            eight = slice(i * 8, i * 8 + 8)
            acc = acc + e_ref[eight, span] * widen(gain_ref[eight, :], CHUNK)
        column = jnp.sum(acc, axis=0, keepdims=True)
        least = jnp.minimum(least, column)
        out_ref[:, span] = jnp.log(column) - v_ref[:, span]
    safe = (
        (jnp.min(total) > 2.0**-60) & (jnp.max(total) < 2.0**60) & (jnp.min(least) > 2.0**-40)
    )

    @pl.when(jnp.logical_not(safe))
    def _():
        def peak(k, carry):
            at = pl.multiple_of(k * TILE, TILE)
            z = scores_of(proj_ref, jobs_ref, at) + v_ref[:, pl.ds(at, TILE)]
            sum_ref[...] = jnp.maximum(sum_ref[...], jnp.max(z, axis=1, keepdims=True))
            return carry

        sum_ref[...] = jnp.full_like(sum_ref, -jnp.inf)
        lax.fori_loop(0, cols // TILE, peak, 0)
        gain_ref[...] = jnp.zeros_like(gain_ref)

        def add(k, carry):
            at = pl.multiple_of(k * TILE, TILE)
            z = scores_of(proj_ref, jobs_ref, at) + v_ref[:, pl.ds(at, TILE)] - sum_ref[:, :1]
            gain_ref[...] = gain_ref[...] + jnp.sum(jnp.exp(z), axis=1, keepdims=True)
            return carry

        lax.fori_loop(0, cols // TILE, add, 0)
        fresh_ref[...] = jnp.log(mass_ref[...]) - (sum_ref[...] + jnp.log(gain_ref[...]))

        def columns(k, carry):
            at = pl.multiple_of(k * TILE, TILE)
            y = scores_of(proj_ref, jobs_ref, at) + fresh_ref[:, :1]
            top = jnp.max(y, axis=0, keepdims=True)
            out_ref[:, pl.ds(at, TILE)] = top + jnp.log(
                jnp.sum(jnp.exp(y - top), axis=0, keepdims=True)
            )
            return carry

        lax.fori_loop(0, cols // TILE, columns, 0)


def first_body(jobs_n, workers_n, *refs):
    job_pieces, refs = refs[: 3 * jobs_n], refs[3 * jobs_n :]
    worker_pieces, refs = refs[:jobs_n], refs[jobs_n:]
    affinity_ref, start_ref, mass_ref, log_total_ref, *refs = refs
    out_ref, fresh_ref, jobs_ref, workers_ref, proj_ref, *scratch = refs
    job, worker = lax.axis_index("job"), lax.axis_index("worker")
    for s in range(jobs_n):
        own, across, other = job_pieces[3 * s : 3 * s + 3]
        size = own.shape[0]
        jobs_ref[pl.ds(pl.multiple_of((s * workers_n + worker) * size, size), size), :] = own[...]
        for mask, piece in ((2, across[...]), (1, other[:size, :]), (3, other[size:, :])):
            peer = worker ^ mask
            jobs_ref[pl.ds(pl.multiple_of((s * workers_n + peer) * size, size), size), :] = piece
    for s in range(jobs_n):
        size = worker_pieces[s].shape[0]
        at = pl.multiple_of((job ^ s) * size, size)
        workers_ref[pl.ds(at, size), :] = worker_pieces[s][...]
    proj_ref[...] = jnp.dot(
        workers_ref[...], affinity_ref[...], preferred_element_type=F32
    ).astype(BF16)
    sweep_rows_and_columns(
        proj_ref, jobs_ref, start_ref, None, mass_ref, out_ref, fresh_ref, scratch
    )
    out_ref[:, jobs_ref.shape[0] :] = log_total_ref[...]


def next_body(workers_n, *refs):
    piece_refs, refs = refs[:workers_n], refs[workers_n:]
    proj_ref, jobs_ref, col_ref, shift_ref, mass_ref, log_total_ref, *refs = refs
    out_ref, fresh_ref, v_ref, *scratch = refs
    v_ref[...] = new_v(col_ref[...], [ref[...] for ref in piece_refs])[0]
    sweep_rows_and_columns(
        proj_ref, jobs_ref, v_ref, shift_ref, mass_ref, out_ref, fresh_ref, scratch
    )
    out_ref[:, jobs_ref.shape[0] :] = log_total_ref[...]


def moment_body(workers_n, *refs):
    piece_refs, refs = refs[:workers_n], refs[workers_n:]
    proj_ref, jobs_ref, workers_ref, col_ref, shift_ref, *refs = refs
    moment_ref, u_ref, v_ref, weighted_ref = refs
    rows, cols = proj_ref.shape[0], jobs_ref.shape[0]
    v, log_total = new_v(col_ref[...], [ref[...] for ref in piece_refs])
    v_ref[...] = v
    weighted_ref[...] = jnp.zeros_like(weighted_ref)

    def add(k, carry):
        at = pl.multiple_of(k * TILE, TILE)
        z = scores_of(proj_ref, jobs_ref, at) + widen(shift_ref[...] - log_total, TILE)
        coupling = jnp.exp(z + v_ref[:, pl.ds(at, TILE)]).astype(BF16)
        weighted_ref[...] = weighted_ref[...] + jnp.dot(
            coupling, jobs_ref[pl.ds(at, TILE), :], preferred_element_type=F32
        )
        return carry

    lax.fori_loop(0, cols // TILE, add, 0, unroll=True)
    weighted = weighted_ref[...]
    high = weighted.astype(BF16)
    rest = weighted - high.astype(F32)
    middle = rest.astype(BF16)
    low = (rest - middle.astype(F32)).astype(BF16)
    parts = lax.dot_general(
        workers_ref[...],
        jnp.concatenate([high, middle, low], axis=1),
        BY_COLUMN,
        preferred_element_type=F32,
    )
    wide = high.shape[1]
    moment_ref[...] = parts[:, :wide] + (parts[:, wide : 2 * wide] + parts[:, 2 * wide :])
    u = shift_ref[...] - log_total
    diagonal = lax.broadcasted_iota(jnp.int32, (LANES, LANES), 0) == lax.broadcasted_iota(
        jnp.int32, (LANES, LANES), 1
    )
    for k in range(rows // LANES):
        block = jnp.where(diagonal, u[k * LANES : (k + 1) * LANES, :], 0.0)
        u_ref[:, k * LANES : (k + 1) * LANES] = jnp.sum(block, axis=0, keepdims=True)


def call(body, name, outs, n_in, scratch):
    vmem = pl.BlockSpec(memory_space=pltpu.VMEM)
    return pl.pallas_call(
        body,
        out_shape=tuple(jax.ShapeDtypeStruct(shape, dtype) for shape, dtype in outs),
        in_specs=[vmem] * n_in,
        out_specs=(vmem,) * len(outs),
        scratch_shapes=[pltpu.VMEM(shape, F32) for shape in scratch],
        compiler_params=pltpu.CompilerParams(vmem_limit_bytes=40 << 20),
        name=name,
    )


def replicated_plan(jobs_n, workers_n):
    def over_job(value):
        return [value] + [swap(value, "job", jobs_n, s) for s in range(1, jobs_n)]

    def over_worker(value):
        return [value] + [swap(value, "worker", workers_n, s) for s in range(1, workers_n)]

    def on_device(worker_feat, job_feat, affinity, worker_mass, job_mass, v_start, observed):
        rows, cols = jobs_n * worker_feat.shape[0], jobs_n * workers_n * job_feat.shape[0]
        feat = worker_feat.shape[1]
        job_pieces = []
        for own in over_job(job_feat):
            across = swap(own, "worker", workers_n, 2)
            other = swap(jnp.concatenate([own, across], axis=0), "worker", workers_n, 1)
            job_pieces += [own, across, other]
        worker_pieces = over_job(worker_feat)
        columns = over_job(jnp.stack([v_start, job_mass]))
        start = jnp.concatenate([piece[0] for piece in columns])[None, :]
        masses = jnp.concatenate([piece[1] for piece in columns])[None, :]
        log_job = jnp.log(masses) - jnp.log(jnp.sum(masses))
        mass = jnp.broadcast_to(worker_mass[:, None], (rows, LANES))
        log_total = jnp.broadcast_to(jnp.log(jnp.sum(worker_mass)), (1, LANES))

        wide, tall = ((1, cols + LANES), F32), ((rows, LANES), F32)
        work = [(rows, cols), (rows, LANES), (rows, LANES)]
        out, shift, jobs, workers, proj = call(
            functools.partial(first_body, jobs_n, workers_n),
            "first",
            [wide, tall, ((cols, feat), BF16), ((rows, feat), BF16), ((rows, feat), BF16)],
            4 * jobs_n + 4,
            work,
        )(*job_pieces, *worker_pieces, affinity, start, mass, log_total)
        for sweep_index in range(1, SWEEPS):
            out, shift = call(
                functools.partial(next_body, workers_n),
                "sweep",
                [wide, tall],
                workers_n + 6,
                [(1, cols)] + work,
            )(*over_worker(out), proj, jobs, log_job, shift, mass, log_total)
        moment, pot_u, pot_v = call(
            functools.partial(moment_body, workers_n),
            "moment",
            [((feat, feat), F32), ((1, rows), F32), ((1, cols), F32)],
            workers_n + 5,
            [(rows, feat)],
        )(*over_worker(out), proj, jobs, workers, log_job, shift)
        moment = sum(over_worker(moment))
        own_jobs = cols // jobs_n
        return (moment - observed, pot_u.reshape(rows), pot_v[0, :own_jobs])

    return on_device


def tiled_plan(jobs_n, workers_n):
    def parts_of(value, axis, size):
        if size & (size - 1) or size > 8:
            gathered = lax.all_gather(value, axis)
            return [gathered[k] for k in range(size)]
        return [value] + [swap(value, axis, size, mask) for mask in range(1, size)]

    def local_lse(scores, axis):
        highest = jnp.max(scores, axis=axis, keepdims=True)
        return jnp.squeeze(highest, axis) + jnp.log(jnp.sum(jnp.exp(scores - highest), axis=axis))

    def on_device(worker_feat, job_feat, affinity, worker_mass, job_mass, v_start, observed):
        jobs_local = lax.all_gather(job_feat, "worker", axis=0, tiled=True)
        workers_local = lax.all_gather(worker_feat, "job", axis=0, tiled=True)
        projected = jnp.dot(workers_local, affinity, preferred_element_type=F32).astype(BF16)
        worker_sum = sum(parts_of(jnp.sum(worker_mass).reshape(1, 1), "worker", workers_n))
        job_sum = sum(parts_of(jnp.sum(job_mass).reshape(1, 1), "job", jobs_n))
        log_worker = jnp.log(worker_mass) - jnp.log(worker_sum[0])
        log_job = jnp.log(job_mass) - jnp.log(job_sum[0])
        tile = lax.dot_general(projected, jobs_local, BY_ROW, preferred_element_type=F32)
        pot_v = v_start
        pot_u = log_worker
        for sweep_index in range(SWEEPS):
            rows = local_lse(tile + pot_v[None, :], 1)
            pot_u = log_worker - merged(parts_of(rows, "job", jobs_n))
            columns = local_lse(tile + pot_u[:, None], 0)
            pot_v = log_job - merged(parts_of(columns, "worker", workers_n))
        coupling = jnp.exp(tile + pot_u[:, None] + pot_v[None, :]).astype(BF16)
        weighted = jnp.dot(coupling, jobs_local, preferred_element_type=F32)
        moment = lax.dot_general(
            workers_local.astype(F32), weighted, BY_COLUMN, precision=lax.Precision.HIGHEST
        )
        moment = sum(parts_of(sum(parts_of(moment, "worker", workers_n)), "job", jobs_n))
        return (moment - observed, pot_u, pot_v)

    return on_device


def solution(mesh):
    placed = (
        P(("market", "worker", "job"), None),
        P(("market", "job", "worker"), None),
        P(),
        P(("market", "worker")),
        P(("market", "job")),
        P(("market", "job")),
        P("market", None),
    )
    jobs_n, workers_n = mesh.shape["job"], mesh.shape["worker"]
    plan = replicated_plan if (jobs_n, workers_n) == (4, 4) else tiled_plan
    return jax.shard_map(
        plan(jobs_n, workers_n),
        mesh=mesh,
        in_specs=placed,
        out_specs=(P("market", None), P(("market", "worker")), P(("market", "job"))),
        check_vma=False,
    )
```

```python
import functools

import jax
import jax.numpy as jnp
from jax import lax
from jax.experimental import pallas as pl
from jax.experimental.pallas import tpu as pltpu
from jax.sharding import PartitionSpec as P


SWEEPS = 3
LANES = 128
TILE = 512
CHUNK = 1024
BY_ROW = (((1,), (1,)), ((), ()))
BY_COLUMN = (((0,), (0,)), ((), ()))
F32 = jnp.float32
BF16 = jnp.bfloat16


def swap(value, axis, size, mask):
    return lax.ppermute(value, axis, [(i, i ^ mask) for i in range(size)])


def widen(value, width):
    return jnp.tile(value, (1, width // LANES))


def merged(pieces):
    highest = functools.reduce(jnp.maximum, pieces)
    return highest + jnp.log(sum(jnp.exp(piece - highest) for piece in pieces))


def new_v(col, pieces):
    cols = col.shape[1]
    both = merged(pieces)
    log_total = both[:, cols : cols + 1]
    return col + log_total - both[:, :cols], log_total


def scores_of(proj_ref, jobs_ref, at):
    return lax.dot_general(
        proj_ref[...], jobs_ref[pl.ds(at, TILE), :], BY_ROW, preferred_element_type=F32
    )


def sweep_rows_and_columns(proj_ref, jobs_ref, v_ref, shift_ref, mass_ref, out_ref, fresh_ref, scratch):
    e_ref, sum_ref, gain_ref = scratch
    rows, cols = proj_ref.shape[0], jobs_ref.shape[0]

    def fast(k, carry):
        at = pl.multiple_of(k * TILE, TILE)
        z = scores_of(proj_ref, jobs_ref, at) + v_ref[:, pl.ds(at, TILE)]
        if shift_ref is not None:
            z = z + widen(shift_ref[...], TILE)
        e = jnp.exp(z)
        e_ref[:, pl.ds(at, TILE)] = e
        part = e[:, :LANES]
        for j in range(1, TILE // LANES):
            part = part + e[:, j * LANES : (j + 1) * LANES]
        sum_ref[...] = sum_ref[...] + part
        return carry

    sum_ref[...] = jnp.zeros_like(sum_ref)
    lax.fori_loop(0, cols // TILE, fast, 0, unroll=True)
    total = jnp.sum(sum_ref[...], axis=1, keepdims=True)
    gain_ref[...] = mass_ref[...] / total
    fresh = jnp.log(gain_ref[...])
    fresh_ref[...] = fresh if shift_ref is None else shift_ref[...] + fresh
    least = jnp.full((1, CHUNK), jnp.inf, F32)
    for k in range(cols // CHUNK):
        span = slice(k * CHUNK, (k + 1) * CHUNK)
        acc = jnp.zeros((8, CHUNK), F32)
        for i in range(rows // 8):
            eight = slice(i * 8, i * 8 + 8)
            acc = acc + e_ref[eight, span] * widen(gain_ref[eight, :], CHUNK)
        column = jnp.sum(acc, axis=0, keepdims=True)
        least = jnp.minimum(least, column)
        out_ref[:, span] = jnp.log(column) - v_ref[:, span]
    safe = (
        (jnp.min(total) > 2.0**-60) & (jnp.max(total) < 2.0**60) & (jnp.min(least) > 2.0**-40)
    )

    @pl.when(jnp.logical_not(safe))
    def _():
        def peak(k, carry):
            at = pl.multiple_of(k * TILE, TILE)
            z = scores_of(proj_ref, jobs_ref, at) + v_ref[:, pl.ds(at, TILE)]
            sum_ref[...] = jnp.maximum(sum_ref[...], jnp.max(z, axis=1, keepdims=True))
            return carry

        sum_ref[...] = jnp.full_like(sum_ref, -jnp.inf)
        lax.fori_loop(0, cols // TILE, peak, 0)
        gain_ref[...] = jnp.zeros_like(gain_ref)

        def add(k, carry):
            at = pl.multiple_of(k * TILE, TILE)
            z = scores_of(proj_ref, jobs_ref, at) + v_ref[:, pl.ds(at, TILE)] - sum_ref[:, :1]
            gain_ref[...] = gain_ref[...] + jnp.sum(jnp.exp(z), axis=1, keepdims=True)
            return carry

        lax.fori_loop(0, cols // TILE, add, 0)
        fresh_ref[...] = jnp.log(mass_ref[...]) - (sum_ref[...] + jnp.log(gain_ref[...]))

        def columns(k, carry):
            at = pl.multiple_of(k * TILE, TILE)
            y = scores_of(proj_ref, jobs_ref, at) + fresh_ref[:, :1]
            top = jnp.max(y, axis=0, keepdims=True)
            out_ref[:, pl.ds(at, TILE)] = top + jnp.log(
                jnp.sum(jnp.exp(y - top), axis=0, keepdims=True)
            )
            return carry

        lax.fori_loop(0, cols // TILE, columns, 0)


def pack_body(workers_hbm, start_hbm, job_mass_hbm, worker_mass_hbm, message_ref, mass_ref, log_total_ref, columns_ref, worker_mass_ref, arrived):
    size, half = workers_hbm.shape[0], start_hbm.shape[0]
    copies = [
        pltpu.make_async_copy(source, target, arrived.at[k])
        for k, (source, target) in enumerate(
            (
                (start_hbm, columns_ref.at[pl.ds(0, half), :]),
                (job_mass_hbm, columns_ref.at[pl.ds(half, half), :]),
                (worker_mass_hbm, worker_mass_ref),
                (workers_hbm, message_ref.at[pl.ds(0, size), :]),
            )
        )
    ]
    for copy in copies:
        copy.start()
    copies[0].wait()
    copies[1].wait()
    rest = columns_ref[...]
    for k in range(3):
        part = rest.astype(BF16)
        message_ref[size + 2 * half * k : size + 2 * half * (k + 1), :] = part
        rest = rest - part.astype(F32)
    copies[2].wait()
    diagonal = diagonal_mask()
    for k in range(worker_mass_ref.shape[0]):
        block = jnp.where(diagonal, worker_mass_ref[k : k + 1, :], 0.0)
        mass_ref[k * LANES : (k + 1) * LANES, :] = jnp.broadcast_to(
            jnp.sum(block, axis=1, keepdims=True), (LANES, LANES)
        )
    log_total_ref[...] = jnp.broadcast_to(
        jnp.log(jnp.sum(worker_mass_ref[...], keepdims=True)), log_total_ref.shape
    )
    copies[3].wait()


def diagonal_mask():
    shape = (LANES, LANES)
    return lax.broadcasted_iota(jnp.int32, shape, 0) == lax.broadcasted_iota(jnp.int32, shape, 1)


def first_body(jobs_n, workers_n, *refs):
    job_pieces, refs = refs[: 3 * jobs_n], refs[3 * jobs_n :]
    messages, refs = refs[:jobs_n], refs[jobs_n:]
    affinity_ref, mass_ref, log_total_ref, *refs = refs
    out_ref, fresh_ref, jobs_ref, workers_ref, proj_ref, col_ref, *refs = refs
    start_ref, *scratch = refs
    job, worker = lax.axis_index("job"), lax.axis_index("worker")
    size = job_pieces[0].shape[0]
    for s in range(jobs_n):
        own, across, other = job_pieces[3 * s : 3 * s + 3]
        for mask, piece in ((0, own[...]), (2, across[...]), (1, other[:size, :]), (3, other[size:, :])):
            at = pl.multiple_of((s * workers_n + (worker ^ mask)) * size, size)
            jobs_ref[pl.ds(at, size), :] = piece
    size = workers_ref.shape[0] // jobs_n
    high = (messages[0].shape[0] - size) // 3
    block = jobs_ref.shape[0] // jobs_n
    for s in range(jobs_n):
        at = pl.multiple_of((job ^ s) * size, size)
        workers_ref[pl.ds(at, size), :] = messages[s][:size, :]
        value = messages[s][size : size + high, :].astype(F32)
        value = value + messages[s][size + high : size + 2 * high, :].astype(F32)
        value = value + messages[s][size + 2 * high :, :].astype(F32)
        for r in range(high // 2):
            lanes = slice(s * block + r * LANES, s * block + (r + 1) * LANES)
            start_ref[:, lanes] = value[r : r + 1, :]
            col_ref[:, lanes] = value[high // 2 + r : high // 2 + r + 1, :]
    col_ref[...] = jnp.log(col_ref[...]) - jnp.log(jnp.sum(col_ref[...], axis=1, keepdims=True))
    proj_ref[...] = jnp.dot(
        workers_ref[...], affinity_ref[...], preferred_element_type=F32
    ).astype(BF16)
    sweep_rows_and_columns(
        proj_ref, jobs_ref, start_ref, None, mass_ref, out_ref, fresh_ref, scratch
    )
    out_ref[:, jobs_ref.shape[0] :] = log_total_ref[...]


def next_body(workers_n, *refs):
    piece_refs, refs = refs[:workers_n], refs[workers_n:]
    proj_ref, jobs_ref, col_ref, shift_ref, mass_ref, log_total_ref, *refs = refs
    out_ref, fresh_ref, v_ref, *scratch = refs
    v_ref[...] = new_v(col_ref[...], [ref[...] for ref in piece_refs])[0]
    sweep_rows_and_columns(
        proj_ref, jobs_ref, v_ref, shift_ref, mass_ref, out_ref, fresh_ref, scratch
    )
    out_ref[:, jobs_ref.shape[0] :] = log_total_ref[...]


def moment_body(workers_n, *refs):
    piece_refs, refs = refs[:workers_n], refs[workers_n:]
    proj_ref, jobs_ref, workers_ref, col_ref, shift_ref, *refs = refs
    moment_ref, u_ref, v_ref, weighted_ref = refs
    rows, cols = proj_ref.shape[0], jobs_ref.shape[0]
    v, log_total = new_v(col_ref[...], [ref[...] for ref in piece_refs])
    v_ref[...] = v
    weighted_ref[...] = jnp.zeros_like(weighted_ref)

    def add(k, carry):
        at = pl.multiple_of(k * TILE, TILE)
        z = scores_of(proj_ref, jobs_ref, at) + widen(shift_ref[...] - log_total, TILE)
        coupling = jnp.exp(z + v_ref[:, pl.ds(at, TILE)]).astype(BF16)
        weighted_ref[...] = weighted_ref[...] + jnp.dot(
            coupling, jobs_ref[pl.ds(at, TILE), :], preferred_element_type=F32
        )
        return carry

    lax.fori_loop(0, cols // TILE, add, 0, unroll=True)
    weighted = weighted_ref[...]
    high = weighted.astype(BF16)
    rest = weighted - high.astype(F32)
    middle = rest.astype(BF16)
    low = (rest - middle.astype(F32)).astype(BF16)
    parts = lax.dot_general(
        workers_ref[...],
        jnp.concatenate([high, middle, low], axis=1),
        BY_COLUMN,
        preferred_element_type=F32,
    )
    wide = high.shape[1]
    moment_ref[...] = parts[:, :wide] + (parts[:, wide : 2 * wide] + parts[:, 2 * wide :])
    u = shift_ref[...] - log_total
    diagonal = diagonal_mask()
    for k in range(rows // LANES):
        block = jnp.where(diagonal, u[k * LANES : (k + 1) * LANES, :], 0.0)
        u_ref[:, k * LANES : (k + 1) * LANES] = jnp.sum(block, axis=0, keepdims=True)


def call(body, outs, n_in, scratch):
    vmem = pl.BlockSpec(memory_space=pltpu.VMEM)
    return pl.pallas_call(
        body,
        out_shape=tuple(jax.ShapeDtypeStruct(shape, dtype) for shape, dtype in outs),
        in_specs=[vmem] * n_in,
        out_specs=(vmem,) * len(outs),
        scratch_shapes=[pltpu.VMEM(shape, F32) for shape in scratch],
        compiler_params=pltpu.CompilerParams(vmem_limit_bytes=40 << 20),
    )


def replicated_plan(jobs_n, workers_n):
    def over_job(value):
        return [value] + [swap(value, "job", jobs_n, s) for s in range(1, jobs_n)]

    def over_worker(value):
        return [value] + [swap(value, "worker", workers_n, s) for s in range(1, workers_n)]

    def on_device(worker_feat, job_feat, affinity, worker_mass, job_mass, v_start, observed):
        rows, cols = jobs_n * worker_feat.shape[0], jobs_n * workers_n * job_feat.shape[0]
        feat = worker_feat.shape[1]
        own_rows, own_cols = worker_feat.shape[0], cols // jobs_n
        high = 2 * (own_cols // LANES)
        wide, tall = ((1, cols + LANES), F32), ((rows, LANES), F32)
        vmem, anywhere = pl.BlockSpec(memory_space=pltpu.VMEM), pl.BlockSpec(memory_space=pl.ANY)
        message, mass, log_total = pl.pallas_call(
            pack_body,
            out_shape=(
                jax.ShapeDtypeStruct((own_rows + 3 * high, feat), BF16),
                jax.ShapeDtypeStruct((rows, LANES), F32),
                jax.ShapeDtypeStruct((1, LANES), F32),
            ),
            in_specs=[anywhere] * 4,
            out_specs=(vmem,) * 3,
            scratch_shapes=[
                pltpu.VMEM((high, LANES), F32),
                pltpu.VMEM((rows // LANES, LANES), F32),
                pltpu.SemaphoreType.DMA((4,)),
            ],
            compiler_params=pltpu.CompilerParams(vmem_limit_bytes=8 << 20),
            name="pack",
        )(
            worker_feat,
            v_start.reshape(-1, LANES),
            job_mass.reshape(-1, LANES),
            worker_mass.reshape(-1, LANES),
        )
        job_pieces = []
        for own in over_job(job_feat):
            across = swap(own, "worker", workers_n, 2)
            both = jnp.concatenate([own, across], axis=0)
            other = swap(both, "worker", workers_n, 1)
            job_pieces += [own, across, other]
        messages = over_job(message)
        work = [(rows, cols), (rows, LANES), (rows, LANES)]
        out, shift, jobs, workers, proj, log_job = call(
            functools.partial(first_body, jobs_n, workers_n),
            [
                wide,
                tall,
                ((cols, feat), BF16),
                ((rows, feat), BF16),
                ((rows, feat), BF16),
                ((1, cols), F32),
            ],
            4 * jobs_n + 3,
            [(1, cols)] + work,
        )(*job_pieces, *messages, affinity, mass, log_total)
        for _ in range(1, SWEEPS):
            out, shift = call(
                functools.partial(next_body, workers_n),
                [wide, tall],
                workers_n + 6,
                [(1, cols)] + work,
            )(*over_worker(out), proj, jobs, log_job, shift, mass, log_total)
        moment, pot_u, pot_v = call(
            functools.partial(moment_body, workers_n),
            [((feat, feat), F32), ((1, rows), F32), ((1, cols), F32)],
            workers_n + 5,
            [(rows, feat)],
        )(*over_worker(out), proj, jobs, workers, log_job, shift)
        moment = sum(over_worker(moment))
        own_jobs = cols // jobs_n
        return (moment - observed, pot_u.reshape(rows), pot_v[0, :own_jobs])

    return on_device


def tiled_plan(jobs_n, workers_n):
    def parts_of(value, axis, size):
        if size & (size - 1) or size > 8:
            gathered = lax.all_gather(value, axis)
            return [gathered[k] for k in range(size)]
        return [value] + [swap(value, axis, size, mask) for mask in range(1, size)]

    def local_lse(scores, axis):
        highest = jnp.max(scores, axis=axis, keepdims=True)
        return jnp.squeeze(highest, axis) + jnp.log(jnp.sum(jnp.exp(scores - highest), axis=axis))

    def on_device(worker_feat, job_feat, affinity, worker_mass, job_mass, v_start, observed):
        jobs_local = lax.all_gather(job_feat, "worker", axis=0, tiled=True)
        workers_local = lax.all_gather(worker_feat, "job", axis=0, tiled=True)
        projected = jnp.dot(workers_local, affinity, preferred_element_type=F32).astype(BF16)
        worker_sum = sum(parts_of(jnp.sum(worker_mass).reshape(1, 1), "worker", workers_n))
        job_sum = sum(parts_of(jnp.sum(job_mass).reshape(1, 1), "job", jobs_n))
        log_worker = jnp.log(worker_mass) - jnp.log(worker_sum[0])
        log_job = jnp.log(job_mass) - jnp.log(job_sum[0])
        tile = lax.dot_general(projected, jobs_local, BY_ROW, preferred_element_type=F32)
        pot_v = v_start
        pot_u = log_worker
        for _ in range(SWEEPS):
            rows = local_lse(tile + pot_v[None, :], 1)
            pot_u = log_worker - merged(parts_of(rows, "job", jobs_n))
            columns = local_lse(tile + pot_u[:, None], 0)
            pot_v = log_job - merged(parts_of(columns, "worker", workers_n))
        coupling = jnp.exp(tile + pot_u[:, None] + pot_v[None, :]).astype(BF16)
        weighted = jnp.dot(coupling, jobs_local, preferred_element_type=F32)
        moment = lax.dot_general(
            workers_local.astype(F32), weighted, BY_COLUMN, precision=lax.Precision.HIGHEST
        )
        moment = sum(parts_of(sum(parts_of(moment, "worker", workers_n)), "job", jobs_n))
        return (moment - observed, pot_u, pot_v)

    return on_device


def solution(mesh):
    placed = (
        P(("market", "worker", "job"), None),
        P(("market", "job", "worker"), None),
        P(),
        P(("market", "worker")),
        P(("market", "job")),
        P(("market", "job")),
        P("market", None),
    )
    jobs_n, workers_n = mesh.shape["job"], mesh.shape["worker"]
    replicated = (jobs_n, workers_n) == (4, 4)
    plan = replicated_plan if replicated else tiled_plan

    def layered(*args):
        return plan(jobs_n, workers_n)(*args)

    return jax.shard_map(
        layered,
        mesh=mesh,
        in_specs=placed,
        out_specs=(P("market", None), P(("market", "worker")), P(("market", "job"))),
        check_vma=False,
    )
```

```python
import functools

import jax
import jax.numpy as jnp
from jax import lax
from jax.experimental import pallas as pl
from jax.experimental.pallas import tpu as pltpu
from jax.sharding import PartitionSpec as P


SWEEPS = 3
LANES = 128
TILE = 1024
CHUNK = 1024
BY_ROW = (((1,), (1,)), ((), ()))
BY_COLUMN = (((0,), (0,)), ((), ()))
F32 = jnp.float32
BF16 = jnp.bfloat16


def swap(value, axis, size, mask):
    return lax.ppermute(value, axis, [(i, i ^ mask) for i in range(size)])


def widen(value, width):
    return jnp.tile(value, (1, width // LANES))


def merged(pieces):
    highest = functools.reduce(jnp.maximum, pieces)
    return highest + jnp.log(sum(jnp.exp(piece - highest) for piece in pieces))


def new_v(col, pieces):
    cols = col.shape[1]
    both = merged(pieces)
    log_total = both[:, cols : cols + 1]
    return col + log_total - both[:, :cols], log_total


def scores_of(rows_ref, jobs_ref, at):
    jobs = jobs_ref[pl.ds(at, TILE), :]
    if rows_ref.shape[1] > jobs.shape[1]:
        jobs = jnp.concatenate([jobs, jnp.ones_like(jobs)], axis=1)
    return lax.dot_general(rows_ref[...], jobs, BY_ROW, preferred_element_type=F32)


def with_shift(rows_ref, proj_ref, shift):
    feat = proj_ref.shape[1]
    lane = lax.broadcasted_iota(jnp.int32, shift.shape, 1)
    parts = jnp.zeros_like(shift)
    for k in range(3):
        part = shift.astype(BF16).astype(F32)
        parts = jnp.where(lane == k, part, parts)
        shift = shift - part
    rows_ref[:, :feat] = proj_ref[...]
    rows_ref[:, feat:] = parts.astype(BF16)


def sweep_rows_and_columns(proj_ref, jobs_ref, v_ref, shift_ref, mass_ref, out_ref, fresh_ref, scratch):
    e_ref, sum_ref, gain_ref, *shifted = scratch
    rows, cols = proj_ref.shape[0], jobs_ref.shape[0]
    rows_ref = proj_ref
    if shift_ref is not None:
        (rows_ref,) = shifted
        with_shift(rows_ref, proj_ref, shift_ref[...])

    def fast(k, carry):
        at = pl.multiple_of(k * TILE, TILE)
        e = jnp.exp(scores_of(rows_ref, jobs_ref, at) + v_ref[:, pl.ds(at, TILE)])
        e_ref[:, pl.ds(at, TILE)] = e
        part = e[:, :LANES]
        for j in range(1, TILE // LANES):
            part = part + e[:, j * LANES : (j + 1) * LANES]
        sum_ref[...] = sum_ref[...] + part
        return carry

    sum_ref[...] = jnp.zeros_like(sum_ref)
    lax.fori_loop(0, cols // TILE, fast, 0, unroll=True)
    total = jnp.sum(sum_ref[...], axis=1, keepdims=True)
    gain_ref[...] = mass_ref[...] / total
    fresh = jnp.log(gain_ref[...])
    fresh_ref[...] = fresh if shift_ref is None else shift_ref[...] + fresh
    least = jnp.full((1, CHUNK), jnp.inf, F32)
    for k in range(cols // CHUNK):
        span = slice(k * CHUNK, (k + 1) * CHUNK)
        acc = jnp.zeros((8, CHUNK), F32)
        for i in range(rows // 8):
            eight = slice(i * 8, i * 8 + 8)
            acc = acc + e_ref[eight, span] * widen(gain_ref[eight, :], CHUNK)
        column = jnp.sum(acc, axis=0, keepdims=True)
        least = jnp.minimum(least, column)
        out_ref[:, span] = jnp.log(column) - v_ref[:, span]
    safe = (
        (jnp.min(total) > 2.0**-60) & (jnp.max(total) < 2.0**60) & (jnp.min(least) > 2.0**-40)
    )

    @pl.when(jnp.logical_not(safe))
    def _():
        def peak(k, carry):
            at = pl.multiple_of(k * TILE, TILE)
            z = scores_of(proj_ref, jobs_ref, at) + v_ref[:, pl.ds(at, TILE)]
            sum_ref[...] = jnp.maximum(sum_ref[...], jnp.max(z, axis=1, keepdims=True))
            return carry

        sum_ref[...] = jnp.full_like(sum_ref, -jnp.inf)
        lax.fori_loop(0, cols // TILE, peak, 0)
        gain_ref[...] = jnp.zeros_like(gain_ref)

        def add(k, carry):
            at = pl.multiple_of(k * TILE, TILE)
            z = scores_of(proj_ref, jobs_ref, at) + v_ref[:, pl.ds(at, TILE)] - sum_ref[:, :1]
            gain_ref[...] = gain_ref[...] + jnp.sum(jnp.exp(z), axis=1, keepdims=True)
            return carry

        lax.fori_loop(0, cols // TILE, add, 0)
        fresh_ref[...] = jnp.log(mass_ref[...]) - (sum_ref[...] + jnp.log(gain_ref[...]))

        def columns(k, carry):
            at = pl.multiple_of(k * TILE, TILE)
            y = scores_of(proj_ref, jobs_ref, at) + fresh_ref[:, :1]
            top = jnp.max(y, axis=0, keepdims=True)
            out_ref[:, pl.ds(at, TILE)] = top + jnp.log(
                jnp.sum(jnp.exp(y - top), axis=0, keepdims=True)
            )
            return carry

        lax.fori_loop(0, cols // TILE, columns, 0)


def pack_body(workers_hbm, start_hbm, job_mass_hbm, worker_mass_hbm, message_ref, mass_ref, log_total_ref, columns_ref, worker_mass_ref, arrived):
    size, half = workers_hbm.shape[0], start_hbm.shape[0]
    copies = [
        pltpu.make_async_copy(source, target, arrived.at[k])
        for k, (source, target) in enumerate(
            (
                (start_hbm, columns_ref.at[pl.ds(0, half), :]),
                (job_mass_hbm, columns_ref.at[pl.ds(half, half), :]),
                (worker_mass_hbm, worker_mass_ref),
                (workers_hbm, message_ref.at[pl.ds(0, size), :]),
            )
        )
    ]
    for copy in copies:
        copy.start()
    copies[0].wait()
    copies[1].wait()
    rest = columns_ref[...]
    for k in range(3):
        part = rest.astype(BF16)
        message_ref[size + 2 * half * k : size + 2 * half * (k + 1), :] = part
        rest = rest - part.astype(F32)
    copies[2].wait()
    diagonal = diagonal_mask()
    for k in range(worker_mass_ref.shape[0]):
        block = jnp.where(diagonal, worker_mass_ref[k : k + 1, :], 0.0)
        mass_ref[k * LANES : (k + 1) * LANES, :] = jnp.broadcast_to(
            jnp.sum(block, axis=1, keepdims=True), (LANES, LANES)
        )
    log_total_ref[...] = jnp.broadcast_to(
        jnp.log(jnp.sum(worker_mass_ref[...], keepdims=True)), log_total_ref.shape
    )
    copies[3].wait()


def diagonal_mask():
    shape = (LANES, LANES)
    return lax.broadcasted_iota(jnp.int32, shape, 0) == lax.broadcasted_iota(jnp.int32, shape, 1)


def first_body(jobs_n, workers_n, *refs):
    job_pieces, refs = refs[:8], refs[8:]
    messages, refs = refs[:jobs_n], refs[jobs_n:]
    affinity_ref, mass_ref, log_total_ref, *refs = refs
    out_ref, fresh_ref, jobs_ref, workers_ref, proj_ref, col_ref, *refs = refs
    start_ref, *scratch = refs
    job, worker = lax.axis_index("job"), lax.axis_index("worker")
    size = job_pieces[0].shape[0]
    for mask in range(4):
        own, others = job_pieces[mask], job_pieces[4 + mask]
        for s in range(jobs_n):
            block = own[...] if s == 0 else others[(s - 1) * size : s * size, :]
            at = pl.multiple_of((s * workers_n + (worker ^ mask)) * size, size)
            jobs_ref[pl.ds(at, size), :] = block
    size = workers_ref.shape[0] // jobs_n
    high = (messages[0].shape[0] - size) // 3
    block = jobs_ref.shape[0] // jobs_n
    for s in range(jobs_n):
        at = pl.multiple_of((job ^ s) * size, size)
        workers_ref[pl.ds(at, size), :] = messages[s][:size, :]
        value = messages[s][size : size + high, :].astype(F32)
        value = value + messages[s][size + high : size + 2 * high, :].astype(F32)
        value = value + messages[s][size + 2 * high :, :].astype(F32)
        for r in range(high // 2):
            lanes = slice(s * block + r * LANES, s * block + (r + 1) * LANES)
            start_ref[:, lanes] = value[r : r + 1, :]
            col_ref[:, lanes] = value[high // 2 + r : high // 2 + r + 1, :]
    col_ref[...] = jnp.log(col_ref[...]) - jnp.log(jnp.sum(col_ref[...], axis=1, keepdims=True))
    proj_ref[...] = jnp.dot(
        workers_ref[...], affinity_ref[...], preferred_element_type=F32
    ).astype(BF16)
    sweep_rows_and_columns(
        proj_ref, jobs_ref, start_ref, None, mass_ref, out_ref, fresh_ref, scratch
    )
    out_ref[:, jobs_ref.shape[0] :] = log_total_ref[...]


def next_body(workers_n, *refs):
    piece_refs, refs = refs[:workers_n], refs[workers_n:]
    proj_ref, jobs_ref, col_ref, shift_ref, mass_ref, log_total_ref, *refs = refs
    out_ref, fresh_ref, v_ref, *scratch = refs
    v_ref[...] = new_v(col_ref[...], [ref[...] for ref in piece_refs])[0]
    sweep_rows_and_columns(
        proj_ref, jobs_ref, v_ref, shift_ref, mass_ref, out_ref, fresh_ref, scratch
    )
    out_ref[:, jobs_ref.shape[0] :] = log_total_ref[...]


def moment_body(workers_n, *refs):
    piece_refs, refs = refs[:workers_n], refs[workers_n:]
    proj_ref, jobs_ref, workers_ref, col_ref, shift_ref, *refs = refs
    moment_ref, u_ref, v_ref, weighted_ref, rows_ref = refs
    rows, cols = proj_ref.shape[0], jobs_ref.shape[0]
    v, log_total = new_v(col_ref[...], [ref[...] for ref in piece_refs])
    v_ref[...] = v
    weighted_ref[...] = jnp.zeros_like(weighted_ref)
    u = shift_ref[...] - log_total
    with_shift(rows_ref, proj_ref, u)

    def add(k, carry):
        at = pl.multiple_of(k * TILE, TILE)
        z = scores_of(rows_ref, jobs_ref, at) + v_ref[:, pl.ds(at, TILE)]
        weighted_ref[...] = weighted_ref[...] + jnp.dot(
            jnp.exp(z).astype(BF16), jobs_ref[pl.ds(at, TILE), :], preferred_element_type=F32
        )
        return carry

    lax.fori_loop(0, cols // TILE, add, 0, unroll=True)
    weighted = weighted_ref[...]
    high = weighted.astype(BF16)
    rest = weighted - high.astype(F32)
    middle = rest.astype(BF16)
    low = (rest - middle.astype(F32)).astype(BF16)
    parts = lax.dot_general(
        workers_ref[...],
        jnp.concatenate([high, middle, low], axis=1),
        BY_COLUMN,
        preferred_element_type=F32,
    )
    wide = high.shape[1]
    moment_ref[...] = parts[:, :wide] + (parts[:, wide : 2 * wide] + parts[:, 2 * wide :])
    diagonal = diagonal_mask()
    for k in range(rows // LANES):
        block = jnp.where(diagonal, u[k * LANES : (k + 1) * LANES, :], 0.0)
        u_ref[:, k * LANES : (k + 1) * LANES] = jnp.sum(block, axis=0, keepdims=True)


def call(body, outs, n_in, scratch, rows_shape=None):
    vmem = pl.BlockSpec(memory_space=pltpu.VMEM)
    return pl.pallas_call(
        body,
        out_shape=tuple(jax.ShapeDtypeStruct(shape, dtype) for shape, dtype in outs),
        in_specs=[vmem] * n_in,
        out_specs=(vmem,) * len(outs),
        scratch_shapes=[pltpu.VMEM(shape, F32) for shape in scratch]
        + ([pltpu.VMEM(rows_shape, BF16)] if rows_shape else []),
        compiler_params=pltpu.CompilerParams(vmem_limit_bytes=40 << 20),
    )


def replicated_plan(jobs_n, workers_n):
    def over_job(value):
        return [value] + [swap(value, "job", jobs_n, s) for s in range(1, jobs_n)]

    def over_worker(value):
        return [value] + [swap(value, "worker", workers_n, s) for s in range(1, workers_n)]

    def on_device(worker_feat, job_feat, affinity, worker_mass, job_mass, v_start, observed):
        rows, cols = jobs_n * worker_feat.shape[0], jobs_n * workers_n * job_feat.shape[0]
        feat = worker_feat.shape[1]
        own_rows, own_cols = worker_feat.shape[0], cols // jobs_n
        high = 2 * (own_cols // LANES)
        wide, tall = ((1, cols + LANES), F32), ((rows, LANES), F32)
        vmem, anywhere = pl.BlockSpec(memory_space=pltpu.VMEM), pl.BlockSpec(memory_space=pl.ANY)
        message, mass, log_total = pl.pallas_call(
            pack_body,
            out_shape=(
                jax.ShapeDtypeStruct((own_rows + 3 * high, feat), BF16),
                jax.ShapeDtypeStruct((rows, LANES), F32),
                jax.ShapeDtypeStruct((1, LANES), F32),
            ),
            in_specs=[anywhere] * 4,
            out_specs=(vmem,) * 3,
            scratch_shapes=[
                pltpu.VMEM((high, LANES), F32),
                pltpu.VMEM((rows // LANES, LANES), F32),
                pltpu.SemaphoreType.DMA((4,)),
            ],
            compiler_params=pltpu.CompilerParams(vmem_limit_bytes=8 << 20),
            name="pack",
        )(
            worker_feat,
            v_start.reshape(-1, LANES),
            job_mass.reshape(-1, LANES),
            worker_mass.reshape(-1, LANES),
        )
        job_pieces = []
        own, *others = over_job(job_feat)
        for held in (own, jnp.concatenate(others, axis=0)):
            across = swap(held, "worker", workers_n, 2)
            job_pieces += [held, swap(held, "worker", workers_n, 1)]
            job_pieces += [across, swap(across, "worker", workers_n, 1)]
        messages = over_job(message)
        work = [(rows, cols), (rows, LANES), (rows, LANES)]
        out, shift, jobs, workers, proj, log_job = call(
            functools.partial(first_body, jobs_n, workers_n),
            [
                wide,
                tall,
                ((cols, feat), BF16),
                ((rows, feat), BF16),
                ((rows, feat), BF16),
                ((1, cols), F32),
            ],
            jobs_n + 11,
            [(1, cols)] + work,
        )(*job_pieces, *messages, affinity, mass, log_total)
        for _ in range(1, SWEEPS):
            out, shift = call(
                functools.partial(next_body, workers_n),
                [wide, tall],
                workers_n + 6,
                [(1, cols)] + work,
                (rows, 2 * feat),
            )(*over_worker(out), proj, jobs, log_job, shift, mass, log_total)
        moment, pot_u, pot_v = call(
            functools.partial(moment_body, workers_n),
            [((feat, feat), F32), ((1, rows), F32), ((1, cols), F32)],
            workers_n + 5,
            [(rows, feat)],
            (rows, 2 * feat),
        )(*over_worker(out), proj, jobs, workers, log_job, shift)
        moment = sum(over_worker(moment))
        own_jobs = cols // jobs_n
        return (moment - observed, pot_u.reshape(rows), pot_v[0, :own_jobs])

    return on_device


def tiled_plan(jobs_n, workers_n):
    def parts_of(value, axis, size):
        if size & (size - 1) or size > 8:
            gathered = lax.all_gather(value, axis)
            return [gathered[k] for k in range(size)]
        return [value] + [swap(value, axis, size, mask) for mask in range(1, size)]

    def local_lse(scores, axis):
        highest = jnp.max(scores, axis=axis, keepdims=True)
        return jnp.squeeze(highest, axis) + jnp.log(jnp.sum(jnp.exp(scores - highest), axis=axis))

    def on_device(worker_feat, job_feat, affinity, worker_mass, job_mass, v_start, observed):
        jobs_local = lax.all_gather(job_feat, "worker", axis=0, tiled=True)
        workers_local = lax.all_gather(worker_feat, "job", axis=0, tiled=True)
        projected = jnp.dot(workers_local, affinity, preferred_element_type=F32).astype(BF16)
        worker_sum = sum(parts_of(jnp.sum(worker_mass).reshape(1, 1), "worker", workers_n))
        job_sum = sum(parts_of(jnp.sum(job_mass).reshape(1, 1), "job", jobs_n))
        log_worker = jnp.log(worker_mass) - jnp.log(worker_sum[0])
        log_job = jnp.log(job_mass) - jnp.log(job_sum[0])
        tile = lax.dot_general(projected, jobs_local, BY_ROW, preferred_element_type=F32)
        pot_v = v_start
        pot_u = log_worker
        for _ in range(SWEEPS):
            rows = local_lse(tile + pot_v[None, :], 1)
            pot_u = log_worker - merged(parts_of(rows, "job", jobs_n))
            columns = local_lse(tile + pot_u[:, None], 0)
            pot_v = log_job - merged(parts_of(columns, "worker", workers_n))
        coupling = jnp.exp(tile + pot_u[:, None] + pot_v[None, :]).astype(BF16)
        weighted = jnp.dot(coupling, jobs_local, preferred_element_type=F32)
        moment = lax.dot_general(
            workers_local.astype(F32), weighted, BY_COLUMN, precision=lax.Precision.HIGHEST
        )
        moment = sum(parts_of(sum(parts_of(moment, "worker", workers_n)), "job", jobs_n))
        return (moment - observed, pot_u, pot_v)

    return on_device


def solution(mesh):
    placed = (
        P(("market", "worker", "job"), None),
        P(("market", "job", "worker"), None),
        P(),
        P(("market", "worker")),
        P(("market", "job")),
        P(("market", "job")),
        P("market", None),
    )
    jobs_n, workers_n = mesh.shape["job"], mesh.shape["worker"]
    replicated = (jobs_n, workers_n) == (4, 4)
    plan = replicated_plan if replicated else tiled_plan

    def layered(*args):
        return plan(jobs_n, workers_n)(*args)

    return jax.shard_map(
        layered,
        mesh=mesh,
        in_specs=placed,
        out_specs=(P("market", None), P(("market", "worker")), P(("market", "job"))),
        check_vma=False,
    )
```

```python
import functools

import jax
import jax.numpy as jnp
from jax import lax
from jax.experimental import pallas as pl
from jax.experimental.pallas import tpu as pltpu
from jax.sharding import PartitionSpec as P


SWEEPS = 3
LANES = 128
TILE = 1024
CHUNK = 1024
BY_ROW = (((1,), (1,)), ((), ()))
BY_COLUMN = (((0,), (0,)), ((), ()))
F32 = jnp.float32
BF16 = jnp.bfloat16


def swap(value, axis, size, mask):
    return lax.ppermute(value, axis, [(i, i ^ mask) for i in range(size)])


def thirds_of(rest):
    thirds = []
    for _ in range(3):
        part = lax.reduce_precision(rest, 8, 7)
        thirds.append(part.astype(BF16))
        rest = rest - part
    return thirds


def widen(value, width):
    return jnp.tile(value, (1, width // LANES))


def merged(pieces):
    highest = functools.reduce(jnp.maximum, pieces)
    return highest + jnp.log(sum(jnp.exp(piece - highest) for piece in pieces))


def new_v(col, pieces):
    cols = col.shape[1]
    both = merged(pieces)
    log_total = both[:, cols : cols + 1]
    return col + log_total - both[:, :cols], log_total


def scores_of(rows_ref, jobs_ref, at):
    jobs = jobs_ref[pl.ds(at, TILE), :]
    if rows_ref.shape[1] > jobs.shape[1]:
        jobs = jnp.concatenate([jobs, jnp.ones_like(jobs)], axis=1)
    return lax.dot_general(rows_ref[...], jobs, BY_ROW, preferred_element_type=F32)


def with_shift(rows_ref, proj_ref, shift):
    feat = proj_ref.shape[1]
    lane = lax.broadcasted_iota(jnp.int32, shift.shape, 1)
    parts = jnp.zeros_like(shift)
    for k in range(3):
        part = shift.astype(BF16).astype(F32)
        parts = jnp.where(lane == k, part, parts)
        shift = shift - part
    rows_ref[:, :feat] = proj_ref[...]
    rows_ref[:, feat:] = parts.astype(BF16)


def sweep_rows_and_columns(proj_ref, jobs_ref, v_ref, shift_ref, mass_ref, out_ref, fresh_ref, scratch):
    e_ref, sum_ref, gain_ref, *shifted = scratch
    rows, cols = proj_ref.shape[0], jobs_ref.shape[0]
    rows_ref = proj_ref
    if shift_ref is not None:
        (rows_ref,) = shifted
        with_shift(rows_ref, proj_ref, shift_ref[...])

    def fast(k, carry):
        at = pl.multiple_of(k * TILE, TILE)
        e = jnp.exp(scores_of(rows_ref, jobs_ref, at) + v_ref[:, pl.ds(at, TILE)])
        e_ref[:, pl.ds(at, TILE)] = e
        part = e[:, :LANES]
        for j in range(1, TILE // LANES):
            part = part + e[:, j * LANES : (j + 1) * LANES]
        sum_ref[...] = sum_ref[...] + part
        return carry

    sum_ref[...] = jnp.zeros_like(sum_ref)
    lax.fori_loop(0, cols // TILE, fast, 0, unroll=True)
    total = jnp.sum(sum_ref[...], axis=1, keepdims=True)
    gain_ref[...] = mass_ref[...] / total
    fresh = jnp.log(gain_ref[...])
    fresh_ref[...] = fresh if shift_ref is None else shift_ref[...] + fresh
    least = jnp.full((1, CHUNK), jnp.inf, F32)
    for k in range(cols // CHUNK):
        span = slice(k * CHUNK, (k + 1) * CHUNK)
        acc = jnp.zeros((8, CHUNK), F32)
        for i in range(rows // 8):
            eight = slice(i * 8, i * 8 + 8)
            acc = acc + e_ref[eight, span] * widen(gain_ref[eight, :], CHUNK)
        column = jnp.sum(acc, axis=0, keepdims=True)
        least = jnp.minimum(least, column)
        out_ref[:, span] = jnp.log(column) - v_ref[:, span]
    safe = (
        (jnp.min(total) > 2.0**-60) & (jnp.max(total) < 2.0**60) & (jnp.min(least) > 2.0**-40)
    )

    @pl.when(jnp.logical_not(safe))
    def _():
        def peak(k, carry):
            at = pl.multiple_of(k * TILE, TILE)
            z = scores_of(proj_ref, jobs_ref, at) + v_ref[:, pl.ds(at, TILE)]
            sum_ref[...] = jnp.maximum(sum_ref[...], jnp.max(z, axis=1, keepdims=True))
            return carry

        sum_ref[...] = jnp.full_like(sum_ref, -jnp.inf)
        lax.fori_loop(0, cols // TILE, peak, 0)
        gain_ref[...] = jnp.zeros_like(gain_ref)

        def add(k, carry):
            at = pl.multiple_of(k * TILE, TILE)
            z = scores_of(proj_ref, jobs_ref, at) + v_ref[:, pl.ds(at, TILE)] - sum_ref[:, :1]
            gain_ref[...] = gain_ref[...] + jnp.sum(jnp.exp(z), axis=1, keepdims=True)
            return carry

        lax.fori_loop(0, cols // TILE, add, 0)
        fresh_ref[...] = jnp.log(mass_ref[...]) - (sum_ref[...] + jnp.log(gain_ref[...]))

        def columns(k, carry):
            at = pl.multiple_of(k * TILE, TILE)
            y = scores_of(proj_ref, jobs_ref, at) + fresh_ref[:, :1]
            top = jnp.max(y, axis=0, keepdims=True)
            out_ref[:, pl.ds(at, TILE)] = top + jnp.log(
                jnp.sum(jnp.exp(y - top), axis=0, keepdims=True)
            )
            return carry

        lax.fori_loop(0, cols // TILE, columns, 0)


def diagonal_mask():
    shape = (LANES, LANES)
    return lax.broadcasted_iota(jnp.int32, shape, 0) == lax.broadcasted_iota(jnp.int32, shape, 1)


def first_body(jobs_n, workers_n, *refs):
    job_pieces, refs = refs[:10], refs[10:]
    third_refs, refs = refs[:3], refs[3:]
    messages, refs = refs[:jobs_n], refs[jobs_n:]
    affinity_ref, *refs = refs
    out_ref, fresh_ref, jobs_ref, workers_ref, proj_ref, col_ref, mass_ref, log_total_ref, *refs = refs
    start_ref, *scratch = refs
    job, worker = lax.axis_index("job"), lax.axis_index("worker")
    size = job_pieces[0].shape[0]
    kept, far, core_own, core_rest, core_far, core_last = job_pieces[:3], job_pieces[3:6], *job_pieces[6:]
    places = (
        [(kept[0], 0), (kept[1], 0)] + [(kept[2], k) for k in range(jobs_n - 2)],
        [(core_own, 0)] + [(core_rest, k) for k in range(jobs_n - 1)],
        [(far[0], 0), (far[1], 0)] + [(far[2], k) for k in range(jobs_n - 2)],
        [(core_far, 0), (core_far, 1)] + [(core_last, k) for k in range(jobs_n - 2)],
    )
    for mask, sources in enumerate(places):
        for s, (source, k) in enumerate(sources):
            at = pl.multiple_of((s * workers_n + (worker ^ mask)) * size, size)
            jobs_ref[pl.ds(at, size), :] = source[k * size : (k + 1) * size, :]
    size = workers_ref.shape[0] // jobs_n
    high = (messages[0].shape[0] - size) // 3
    block = jobs_ref.shape[0] // jobs_n
    for s in range(jobs_n):
        at = pl.multiple_of((job ^ s) * size, size)
        workers_ref[pl.ds(at, size), :] = messages[s][:size, :]
        value = messages[s][size : size + high, :].astype(F32)
        value = value + messages[s][size + high : size + 2 * high, :].astype(F32)
        value = value + messages[s][size + 2 * high :, :].astype(F32)
        for r in range(high // 2):
            lanes = slice(s * block + r * LANES, s * block + (r + 1) * LANES)
            start_ref[:, lanes] = value[r : r + 1, :]
            col_ref[:, lanes] = value[high // 2 + r : high // 2 + r + 1, :]
    col_ref[...] = jnp.log(col_ref[...]) - jnp.log(jnp.sum(col_ref[...], axis=1, keepdims=True))
    worker_mass = sum(ref[high : high + high // 2, :].astype(F32) for ref in third_refs)
    diagonal = diagonal_mask()
    for k in range(worker_mass.shape[0]):
        block_of_mass = jnp.where(diagonal, worker_mass[k : k + 1, :], 0.0)
        mass_ref[k * LANES : (k + 1) * LANES, :] = jnp.broadcast_to(
            jnp.sum(block_of_mass, axis=1, keepdims=True), (LANES, LANES)
        )
    log_total_ref[...] = jnp.broadcast_to(
        jnp.log(jnp.sum(worker_mass, keepdims=True)), log_total_ref.shape
    )
    proj_ref[...] = jnp.dot(
        workers_ref[...], affinity_ref[...], preferred_element_type=F32
    ).astype(BF16)
    sweep_rows_and_columns(
        proj_ref, jobs_ref, start_ref, None, mass_ref, out_ref, fresh_ref, scratch
    )
    out_ref[:, jobs_ref.shape[0] :] = log_total_ref[...]


def next_body(workers_n, *refs):
    piece_refs, refs = refs[:workers_n], refs[workers_n:]
    proj_ref, jobs_ref, col_ref, shift_ref, mass_ref, log_total_ref, *refs = refs
    out_ref, fresh_ref, v_ref, *scratch = refs
    v_ref[...] = new_v(col_ref[...], [ref[...] for ref in piece_refs])[0]
    sweep_rows_and_columns(
        proj_ref, jobs_ref, v_ref, shift_ref, mass_ref, out_ref, fresh_ref, scratch
    )
    out_ref[:, jobs_ref.shape[0] :] = log_total_ref[...]


def moment_body(workers_n, *refs):
    piece_refs, refs = refs[:workers_n], refs[workers_n:]
    proj_ref, jobs_ref, workers_ref, col_ref, shift_ref, *refs = refs
    moment_ref, u_ref, v_ref, weighted_ref, rows_ref = refs
    rows, cols = proj_ref.shape[0], jobs_ref.shape[0]
    v, log_total = new_v(col_ref[...], [ref[...] for ref in piece_refs])
    v_ref[...] = v
    weighted_ref[...] = jnp.zeros_like(weighted_ref)
    u = shift_ref[...] - log_total
    with_shift(rows_ref, proj_ref, u)

    def add(k, carry):
        at = pl.multiple_of(k * TILE, TILE)
        z = scores_of(rows_ref, jobs_ref, at) + v_ref[:, pl.ds(at, TILE)]
        weighted_ref[...] = weighted_ref[...] + jnp.dot(
            jnp.exp(z).astype(BF16), jobs_ref[pl.ds(at, TILE), :], preferred_element_type=F32
        )
        return carry

    lax.fori_loop(0, cols // TILE, add, 0, unroll=True)
    weighted = weighted_ref[...]
    high = weighted.astype(BF16)
    rest = weighted - high.astype(F32)
    middle = rest.astype(BF16)
    low = (rest - middle.astype(F32)).astype(BF16)
    parts = lax.dot_general(
        workers_ref[...],
        jnp.concatenate([high, middle, low], axis=1),
        BY_COLUMN,
        preferred_element_type=F32,
    )
    wide = high.shape[1]
    moment_ref[...] = parts[:, :wide] + (parts[:, wide : 2 * wide] + parts[:, 2 * wide :])
    diagonal = diagonal_mask()
    for k in range(rows // LANES):
        block = jnp.where(diagonal, u[k * LANES : (k + 1) * LANES, :], 0.0)
        u_ref[:, k * LANES : (k + 1) * LANES] = jnp.sum(block, axis=0, keepdims=True)


def call(body, outs, n_in, scratch, rows_shape=None):
    vmem = pl.BlockSpec(memory_space=pltpu.VMEM)
    return pl.pallas_call(
        body,
        out_shape=tuple(jax.ShapeDtypeStruct(shape, dtype) for shape, dtype in outs),
        in_specs=[vmem] * n_in,
        out_specs=(vmem,) * len(outs),
        scratch_shapes=[pltpu.VMEM(shape, F32) for shape in scratch]
        + ([pltpu.VMEM(rows_shape, BF16)] if rows_shape else []),
        compiler_params=pltpu.CompilerParams(vmem_limit_bytes=40 << 20),
    )


def replicated_plan(jobs_n, workers_n):
    def over_job(value):
        return [value] + [swap(value, "job", jobs_n, s) for s in range(1, jobs_n)]

    def over_worker(value):
        return [value] + [swap(value, "worker", workers_n, s) for s in range(1, workers_n)]

    def on_device(worker_feat, job_feat, affinity, worker_mass, job_mass, v_start, observed):
        rows, cols = jobs_n * worker_feat.shape[0], jobs_n * workers_n * job_feat.shape[0]
        feat = worker_feat.shape[1]
        high = 2 * (cols // jobs_n // LANES)
        wide, tall = ((1, cols + LANES), F32), ((rows, LANES), F32)
        by_lanes = [value.reshape(-1, LANES) for value in (v_start, job_mass, worker_mass)]
        thirds = thirds_of(jnp.concatenate(by_lanes + by_lanes[-1:], axis=0))
        message = jnp.concatenate([worker_feat] + [third[:high] for third in thirds], axis=0)
        held = over_job(job_feat)
        held = [held[0], held[1], jnp.concatenate(held[2:], axis=0)]
        across = [swap(one, "worker", workers_n, 2) for one in held]
        job_pieces = held + across
        for pieces in (held[:1], held[1:], across[:2], across[2:]):
            job_pieces.append(swap(jnp.concatenate(pieces, axis=0), "worker", workers_n, 1))
        messages = over_job(message)
        work = [(rows, cols), (rows, LANES), (rows, LANES)]
        out, shift, jobs, workers, proj, log_job, mass, log_total = call(
            functools.partial(first_body, jobs_n, workers_n),
            [
                wide,
                tall,
                ((cols, feat), BF16),
                ((rows, feat), BF16),
                ((rows, feat), BF16),
                ((1, cols), F32),
                tall,
                ((1, LANES), F32),
            ],
            jobs_n + 14,
            [(1, cols)] + work,
        )(*job_pieces, *thirds, *messages, affinity)
        for _ in range(1, SWEEPS):
            out, shift = call(
                functools.partial(next_body, workers_n),
                [wide, tall],
                workers_n + 6,
                [(1, cols)] + work,
                (rows, 2 * feat),
            )(*over_worker(out), proj, jobs, log_job, shift, mass, log_total)
        moment, pot_u, pot_v = call(
            functools.partial(moment_body, workers_n),
            [((feat, feat), F32), ((1, rows), F32), ((1, cols), F32)],
            workers_n + 5,
            [(rows, feat)],
            (rows, 2 * feat),
        )(*over_worker(out), proj, jobs, workers, log_job, shift)
        moment = sum(over_worker(moment))
        own_jobs = cols // jobs_n
        return (moment - observed, pot_u.reshape(rows), pot_v[0, :own_jobs])

    return on_device


def tiled_plan(jobs_n, workers_n):
    def parts_of(value, axis, size):
        if size & (size - 1) or size > 8:
            gathered = lax.all_gather(value, axis)
            return [gathered[k] for k in range(size)]
        return [value] + [swap(value, axis, size, mask) for mask in range(1, size)]

    def local_lse(scores, axis):
        highest = jnp.max(scores, axis=axis, keepdims=True)
        return jnp.squeeze(highest, axis) + jnp.log(jnp.sum(jnp.exp(scores - highest), axis=axis))

    def on_device(worker_feat, job_feat, affinity, worker_mass, job_mass, v_start, observed):
        jobs_local = lax.all_gather(job_feat, "worker", axis=0, tiled=True)
        workers_local = lax.all_gather(worker_feat, "job", axis=0, tiled=True)
        projected = jnp.dot(workers_local, affinity, preferred_element_type=F32).astype(BF16)
        worker_sum = sum(parts_of(jnp.sum(worker_mass).reshape(1, 1), "worker", workers_n))
        job_sum = sum(parts_of(jnp.sum(job_mass).reshape(1, 1), "job", jobs_n))
        log_worker = jnp.log(worker_mass) - jnp.log(worker_sum[0])
        log_job = jnp.log(job_mass) - jnp.log(job_sum[0])
        tile = lax.dot_general(projected, jobs_local, BY_ROW, preferred_element_type=F32)
        pot_v = v_start
        pot_u = log_worker
        for _ in range(SWEEPS):
            rows = local_lse(tile + pot_v[None, :], 1)
            pot_u = log_worker - merged(parts_of(rows, "job", jobs_n))
            columns = local_lse(tile + pot_u[:, None], 0)
            pot_v = log_job - merged(parts_of(columns, "worker", workers_n))
        coupling = jnp.exp(tile + pot_u[:, None] + pot_v[None, :]).astype(BF16)
        weighted = jnp.dot(coupling, jobs_local, preferred_element_type=F32)
        moment = lax.dot_general(
            workers_local.astype(F32), weighted, BY_COLUMN, precision=lax.Precision.HIGHEST
        )
        moment = sum(parts_of(sum(parts_of(moment, "worker", workers_n)), "job", jobs_n))
        return (moment - observed, pot_u, pot_v)

    return on_device


def solution(mesh):
    placed = (
        P(("market", "worker", "job"), None),
        P(("market", "job", "worker"), None),
        P(),
        P(("market", "worker")),
        P(("market", "job")),
        P(("market", "job")),
        P("market", None),
    )
    jobs_n, workers_n = mesh.shape["job"], mesh.shape["worker"]
    replicated = (jobs_n, workers_n) == (4, 4)
    plan = replicated_plan if replicated else tiled_plan

    def layered(*args):
        return plan(jobs_n, workers_n)(*args)

    return jax.shard_map(
        layered,
        mesh=mesh,
        in_specs=placed,
        out_specs=(P("market", None), P(("market", "worker")), P(("market", "job"))),
        check_vma=False,
    )
```
